32 devices in a mesh: blk: 8 (over z, x), road: 4 (over y, core).
Axes of the slice: x: 2, y: 2, z: 4, core: 2. Of those that a mesh axis runs over, the one named last changes fastest.
Arguments:
- disp: float32 [3, 16, 64, 1024], P(None, None, 'road', 'blk'), may hold values from -1.2 to 1.2
- veloc: float32 [3, 16, 64, 1024], P(None, None, 'road', 'blk'), may hold values from -6 to 6
- stiff: float32 [3, 16, 64, 1024], P(None, None, 'road', 'blk'), may hold values from 0.5 to 2
- mass: float32 [16, 64, 1024], P(None, 'road', 'blk'), may hold values from 1 to 4
- road_height: float32 [16384], P('road'), may hold values from -1.2 to 1.2
- road_slope_x: float32 [16384], P('road'), may hold values from -0.3 to 0.3
- road_slope_y: float32 [16384], P('road'), may hold values from -0.3 to 0.3
- road_stiff: float32 [16384], P('road'), may hold values from 1 to 4
- tile_list: int32 [8, 4, 4], P('blk', 'road'), may hold values from 0 to 63, as said below
- pair_node: int32 [8, 4, 8192], P('blk', 'road'), may hold values from 0 to 2047, as said below
- pair_slot: int32 [8, 4, 8192], P('blk', 'road'), may hold values from 0 to 1023, as said below
- pair_count: int32 [8, 4], P('blk', 'road'), may hold values from 0 to 8192, as said below
Outputs:
- veloc_out: float32 [3, 16, 64, 1024], P(None, None, 'road', 'blk')
- road_load: float32 [16384], P(('blk', 'road'))
The draws below stay inside these ranges and needn't reach their ends.
Inputs may be any that keep to these rules, and one draw needn't show every extreme that they name: `pair_count`: the sectors with live slots form one run of 1 consecutive sectors round the cycle, possibly across its end; on their devices from 4096 to 8192 slots are live, and some device has all 8192 live; on all other devices none. Index of a node of the device's own outer layer: lateral position pair_node // 128, circumferential position pair_node % 128 within the device's block. Position within the device's listed tiles: tile pair_slot // 256, facet pair_slot % 256 of that tile. `tile_list`: 4 consecutive tile numbers counted modulo 64; tile t holds facets t * 256 to t * 256 + 255, on road patch t // 16.
All inputs are finite; a program needn't handle non-finite values.
Results may differ from the reference program's by a relative error of at most 0.0001.
Values sent between devices are 32-bit elements; how exact they have to be, the bound alone decides.
A program may use at most 64 MiB of HBM per device.

```python
import math
import jax
import jax.numpy as jnp
from jax import lax

NR = 16
NL = 16
NC = 128
PAIRS = 8192
TILE = 256
TILES_NEED = 4
STEPS = 2
SECTORS = 8
BANDS = 4
CONTACT = 1
FACETS = 16384
TOTAL_TILES = 64
NLT = 64
NCT = 1024


def draw_pair_count(key, part):
    first = jax.random.randint(jax.random.fold_in(key, 11), (), 0, SECTORS)
    sector = jnp.arange(SECTORS, dtype=jnp.int32)
    touching = (sector - first) % SECTORS < CONTACT
    drawn = jax.random.randint(jax.random.fold_in(key, 12), (SECTORS, BANDS), PAIRS // 2, PAIRS + 1).astype(jnp.int32)
    drawn = drawn.at[first, 0].set(PAIRS)
    counts = jnp.where(touching[:, None], drawn, 0)
    return counts.astype(jnp.int32)


def draw_pair_node(key, part):
    drawn = jax.random.randint(jax.random.fold_in(key, 21), (SECTORS, BANDS, PAIRS), 0, NL * NC).astype(jnp.int32)
    return drawn.at[0, 0, 0].set(NL * NC - 1).at[0, 0, 1].set(0)


def draw_pair_slot(key, part):
    drawn = jax.random.randint(jax.random.fold_in(key, 31), (SECTORS, BANDS, PAIRS), 0, TILES_NEED * TILE).astype(jnp.int32)
    return drawn.at[0, 0, 0].set(TILES_NEED * TILE - 1).at[0, 0, 1].set(0)


def draw_tile_list(key, part):
    offsets = jax.random.randint(jax.random.fold_in(key, 41), (SECTORS, BANDS), 0, TOTAL_TILES).astype(jnp.int32)
    offsets = offsets.at[0, 0].set(TOTAL_TILES - 1)
    steps_along = jnp.arange(TILES_NEED, dtype=jnp.int32)
    return ((offsets[:, :, None] + steps_along[None, None, :]) % TOTAL_TILES).astype(jnp.int32)


def level_of(rng, dims, cuts, least, top_value):
    level = 1.0
    for position, blocks in cuts:
        draws = jax.random.uniform(jax.random.fold_in(jax.random.fold_in(rng, 6), position), (blocks,), jnp.float32, least / len(cuts), top_value / len(cuts))
        level = level * jnp.repeat(jnp.exp(draws), dims[position] // blocks).reshape((-1,) + (1,) * (len(dims) - 1 - position))
    return level


def centred(key, dims, scale, limit, cuts=(), kind=jnp.bfloat16):
    array = jax.random.normal(key, dims, jnp.float32) * scale
    if len(cuts) > 0:
        array = level_of(key, dims, cuts, -0.22, 0.18) * array
    return jnp.clip(array, min=-limit, max=limit).astype(kind)


def setup_inputs(seed: int = 0) -> dict:
    splits = jax.random.split(jax.random.key(seed), 13)
    return {
        "disp": centred(splits[0], (3, NR, NLT, NCT), 0.3, 1.2, ((2, 4), (3, 8)), jnp.float32),
        "veloc": centred(splits[1], (3, NR, NLT, NCT), 1.0, 6.0, ((2, 4), (3, 8)), jnp.float32),
        "stiff": jnp.clip(jnp.exp(math.log(2.0) - 1.3862944 * jax.random.uniform(splits[2], (3, NR, NLT, NCT), jnp.float32) ** level_of(splits[2], (3, NR, NLT, NCT), ((2, 4), (3, 8)), -0.2, 0.2)), 0.5, 2.0),
        "mass": jnp.clip(jnp.exp(math.log(4.0) - 1.3862944 * jax.random.uniform(splits[3], (NR, NLT, NCT), jnp.float32) ** level_of(splits[3], (NR, NLT, NCT), ((1, 4), (2, 8)), -0.2, 0.2)), 1.0, 4.0),
        "road_height": centred(splits[4], (FACETS,), 0.3, 1.2, ((0, 4),), jnp.float32),
        "road_slope_x": jnp.clip(jax.random.uniform(splits[5], (FACETS,), jnp.float32, -0.3, 0.3) * level_of(splits[5], (FACETS,), ((0, 4),), -0.4, 0.0), -0.3, 0.3),
        "road_slope_y": jnp.clip(jax.random.uniform(splits[6], (FACETS,), jnp.float32, -0.3, 0.3) * level_of(splits[6], (FACETS,), ((0, 4),), -0.4, 0.0), -0.3, 0.3),
        "road_stiff": jnp.clip(jnp.exp(math.log(4.0) - 1.3862944 * jax.random.uniform(splits[7], (FACETS,), jnp.float32) ** level_of(splits[7], (FACETS,), ((0, 4),), -0.2, 0.2)), 1.0, 4.0),
        "tile_list": draw_tile_list(jax.random.fold_in(splits[12], 71), 0),
        "pair_node": draw_pair_node(jax.random.fold_in(splits[12], 71), 0),
        "pair_slot": draw_pair_slot(jax.random.fold_in(splits[12], 71), 0),
        "pair_count": draw_pair_count(jax.random.fold_in(splits[12], 71), 0),
    }


hardening = 0.5
time_step = 0.25


def stress_term(strain):
    squared = jnp.sum(strain * strain, axis=0, keepdims=True)
    return strain * (1.0 + hardening * squared)


def edge_force(padded, stiff_padded, which_dim):
    length = padded.shape[which_dim]
    strain = lax.slice_in_dim(padded, 1, length, axis=which_dim) - lax.slice_in_dim(padded, 0, length - 1, axis=which_dim)
    weights = lax.slice_in_dim(stiff_padded, 1, length, axis=which_dim - 1)
    tension = weights[None] * stress_term(strain)
    return lax.slice_in_dim(tension, 1, length - 1, axis=which_dim) - lax.slice_in_dim(tension, 0, length - 2, axis=which_dim)


def internal_force(displace, stiffness):
    radial = jnp.pad(displace, ((0, 0), (1, 1), (0, 0), (0, 0)))
    radial_stiff = jnp.pad(stiffness[0], ((1, 1), (0, 0), (0, 0)))
    summed = edge_force(radial, radial_stiff, 1)
    lateral = jnp.pad(displace, ((0, 0), (0, 0), (1, 1), (0, 0)))
    lateral_stiff = jnp.pad(stiffness[1], ((0, 0), (1, 1), (0, 0)))
    summed = summed + edge_force(lateral, lateral_stiff, 2)
    beside_all = jnp.concatenate([displace[..., -1:], displace, displace[..., :1]], axis=3)
    around_stiff = jnp.concatenate([stiffness[2][..., -1:], stiffness[2], stiffness[2][..., :1]], axis=2)
    return summed + edge_force(beside_all, around_stiff, 3)


def press(values):
    return values[6] * jnp.maximum(values[3] + values[4] * values[0] + values[5] * values[1] - values[2], 0.0)


def reference(disp, veloc, stiff, mass, road_height, road_slope_x, road_slope_y, road_stiff, tile_list, pair_node, pair_slot, pair_count):
    lateral_total = NL * BANDS
    around_total = NC * SECTORS
    sector = jnp.arange(SECTORS, dtype=jnp.int32)[:, None, None]
    band_index = jnp.arange(BANDS, dtype=jnp.int32)[None, :, None]
    where_node = ((band_index * NL + pair_node // NC) * around_total + sector * NC + pair_node % NC).reshape(-1)
    tile_pick = jnp.take_along_axis(tile_list, (pair_slot // TILE).astype(jnp.int32), axis=2)
    facet_id = (tile_pick * TILE + pair_slot % TILE).reshape(-1)
    slot_index = jnp.arange(PAIRS, dtype=jnp.int32)[None, None, :]
    live_slots = (slot_index < pair_count[:, :, None]).reshape(-1)
    facet_values = jnp.stack([road_height[facet_id], road_slope_x[facet_id], road_slope_y[facet_id], road_stiff[facet_id]])
    displace = disp
    velocity = veloc
    facet_load = jnp.zeros((FACETS,), jnp.float32)
    for step_index in range(STEPS):
        outer_layer = displace[:, NR - 1].reshape(3, -1)
        picked = outer_layer[:, where_node]
        values = jnp.concatenate([picked, facet_values], axis=0)
        normal_force = jnp.where(live_slots, press(values), 0.0)
        contact = jnp.stack([-values[4] * normal_force, -values[5] * normal_force, normal_force])
        outer_force = jnp.zeros_like(outer_layer).at[:, where_node].add(contact)
        forces = internal_force(displace, stiff)
        forces = forces.at[:, NR - 1].add(outer_force.reshape(3, lateral_total, around_total))
        velocity = velocity + time_step * forces / mass[None]
        displace = displace + time_step * velocity
        facet_load = facet_load + jnp.zeros((FACETS,), jnp.float32).at[facet_id].add(normal_force)
    return velocity, facet_load
```

```python
import functools

import jax
import jax.numpy as jnp
from jax import lax
from jax.experimental import pallas as pl
from jax.experimental.pallas import tpu as pltpu
from jax.sharding import PartitionSpec as P

TILE = 256
LANES = 128
SUB = 8

hardening = 0.5
time_step = 0.25

MESH = pl.DeviceIdType.MESH
NT = (((1,), (1,)), ((), ()))


def split_two(x):
    high = x.astype(jnp.bfloat16).astype(jnp.float32)
    return high, x - high


def tension(weights, strain):
    squared = strain[0] * strain[0] + strain[1] * strain[1] + strain[2] * strain[2]
    scaled = weights * (1.0 + hardening * squared)
    return [scaled * s for s in strain]


def kernel(
    n_blk,
    n_road,
    lat,
    in_kernel_sum,
    disp_in,
    veloc_in,
    stiff_in,
    mass_in,
    height,
    slope_x,
    slope_y,
    road_stiff,
    tiles_in,
    nodes_in,
    slots_in,
    count_in,
    v_out,
    load_out,
    disp,
    veloc,
    stiff,
    mass,
    nodes,
    slots,
    tiles,
    count,
    in_sems,
    own_sems,
    picked,
    facet_vals,
    normals,
    parts,
    u1,
    v1,
    force,
    scale,
    rim,
    side,
    facet_all,
    table,
    up_send,
    down_send,
    up_recv,
    down_recv,
    side_up_send,
    side_down_send,
    side_up_recv,
    side_down_recv,
    halo_sems,
    facet_sems,
    *reduction,
):
    b = lax.axis_index("blk")
    r = lax.axis_index("road")
    rows = disp.shape[1]
    layers = rows // lat
    groups = nodes.shape[0] // SUB
    n_rows = table.shape[1]
    tiles_need = tiles.shape[1]
    half = n_rows // tiles_need
    patch_rows = height.shape[0]

    def road_peer(offset):
        return {"blk": b, "road": lax.rem(r + offset, n_road)}

    def blk_peer(offset):
        return {"blk": lax.rem(b + offset, n_blk), "road": r}

    blk_offsets = range(1, n_blk) if in_kernel_sum else sorted({1, n_blk - 1})
    barrier = pltpu.get_barrier_semaphore()
    for offset in reversed(blk_offsets):
        pl.semaphore_signal(barrier, inc=1, device_id=blk_peer(offset), device_id_type=MESH)
    for offset in range(1, n_road):
        pl.semaphore_signal(barrier, inc=1, device_id=road_peer(offset), device_id_type=MESH)

    def fill_faces(step, source):
        for c in range(3):
            turned = source[c].T
            up_send[step, c : c + 1, :] = turned[LANES - 1 : LANES, :]
            down_send[step, c : c + 1, :] = turned[0:1, :]
            side_up_send[step, c] = source[c, pl.ds(lat - 1, layers, stride=lat), :]
            side_down_send[step, c] = source[c, pl.ds(0, layers, stride=lat), :]
        if step == 0:
            down_send[step, 3:4, :] = stiff[2].T[0:1, :]
            side_down_send[step, 3] = stiff[1, pl.ds(0, layers, stride=lat), :]

    def halo_copies(step):
        plan = (
            (up_send, up_recv, blk_peer(1)),
            (down_send, down_recv, blk_peer(n_blk - 1)),
            (side_up_send, side_up_recv, road_peer(1)),
            (side_down_send, side_down_recv, road_peer(n_road - 1)),
        )
        return [
            pltpu.make_async_remote_copy(
                src_ref=src.at[step],
                dst_ref=dst.at[step],
                send_sem=halo_sems.at[step, 0, i],
                recv_sem=halo_sems.at[step, 1, i],
                device_id=peer,
                device_id_type=MESH,
            )
            for i, (src, dst, peer) in enumerate(plan)
        ]

    loads_in = [
        pltpu.make_async_copy(src, dst, in_sems.at[i])
        for i, (src, dst) in enumerate(
            (
                (disp_in, disp),
                (stiff_in, stiff),
                (nodes_in, nodes),
                (mass_in, mass),
                (veloc_in, veloc),
                (slots_in, slots),
                (tiles_in, tiles),
                (count_in, count),
            )
        )
    ]
    for copy in loads_in:
        copy.start()
    own = (height, slope_x, slope_y, road_stiff)
    own_copies = [
        pltpu.make_async_copy(own[a], facet_all.at[a * n_road + r], own_sems.at[a]) for a in range(4)
    ]
    if in_kernel_sum:
        tiles_all, loads_all, reduced, blk_recv, tile_sems, road_sems, blk_sems = reduction
        own_copies.append(pltpu.make_async_copy(tiles_in, tiles_all.at[r], own_sems.at[4]))
    for copy in own_copies:
        copy.start()
    for copy in loads_in[:2]:
        copy.wait()
    fill_faces(0, disp)

    pl.semaphore_wait(barrier, len(blk_offsets) + n_road - 1)
    halos0 = halo_copies(0)
    for copy in halos0[:2]:
        copy.start()
    facet_copies = []
    for a in range(4):
        for offset in range(1, n_road):
            copy = pltpu.make_async_remote_copy(
                src_ref=own[a],
                dst_ref=facet_all.at[a * n_road + r],
                send_sem=facet_sems.at[0, a, offset - 1],
                recv_sem=facet_sems.at[1, a, offset - 1],
                device_id=road_peer(offset),
                device_id_type=MESH,
            )
            copy.start()
            facet_copies.append(copy)
    for copy in halos0[2:]:
        copy.start()
    tile_copies = []
    if in_kernel_sum:
        for offset in range(1, n_road):
            copy = pltpu.make_async_remote_copy(
                src_ref=tiles_in,
                dst_ref=tiles_all.at[r],
                send_sem=tile_sems.at[0, offset - 1],
                recv_sem=tile_sems.at[1, offset - 1],
                device_id=road_peer(offset),
                device_id_type=MESH,
            )
            copy.start()
            tile_copies.append(copy)

    lat_index = lax.broadcasted_iota(jnp.int32, (lat, LANES), 0)
    lane_index = lax.broadcasted_iota(jnp.int32, (lat, LANES), 1)

    def layer_rows(k):
        return pl.ds(pl.multiple_of(k * lat, lat), lat)

    def inside(source, k, above, bottom):
        at = layer_rows(k)
        u = [source[c, at, :] for c in range(3)]
        if bottom:
            strain = u
        else:
            below = layer_rows(k - 1)
            strain = [u[c] - source[c, below, :] for c in range(3)]
        radial = tension(stiff[0, at, :], strain)
        beside = tension(stiff[1, at, :], [x - pltpu.roll(x, 1, 0) for x in u])
        around = tension(stiff[2, at, :], [x - pltpu.roll(x, 1, 1) for x in u])
        for c in range(3):
            t = jnp.where(lat_index == 0, 0.0, beside[c])
            w = jnp.where(lane_index == 0, 0.0, around[c])
            force[c, at, :] = (
                (above[c] - radial[c])
                + (pltpu.roll(t, lat - 1, 0) - t)
                + (pltpu.roll(w, LANES - 1, 1) - w)
            )
        return radial

    def interior(source):
        nothing = tuple(jnp.zeros((lat, LANES), jnp.float32) for _ in range(3))

        def body(i, above):
            return tuple(inside(source, layers - 1 - i, above, False))

        above = lax.fori_loop(0, layers - 1, body, nothing, unroll=3)
        inside(source, 0, above, True)

    def fill_rim(step):
        stiff_around = down_recv[0, 3:4, :]
        own_around = down_send[0, 3:4, :]
        low = tension(own_around, [down_send[step, c : c + 1, :] - up_recv[step, c : c + 1, :] for c in range(3)])
        high = tension(stiff_around, [down_recv[step, c : c + 1, :] - up_send[step, c : c + 1, :] for c in range(3)])
        for c in range(3):
            for i in range(rows // LANES):
                piece = slice(i * LANES, (i + 1) * LANES)
                rim[c, i : i + 1, :] = -low[c][:, piece]
                rim[3 + c, i : i + 1, :] = high[c][:, piece]
        first = jnp.where(r == 0, 0.0, 1.0)
        last = jnp.where(r == n_road - 1, 0.0, 1.0)
        low = tension(
            side_down_send[0, 3], [side_down_send[step, c] - first * side_up_recv[step, c] for c in range(3)]
        )
        high = tension(
            last * side_down_recv[0, 3], [side_down_recv[step, c] - side_up_send[step, c] for c in range(3)]
        )
        for c in range(3):
            side[c] = -low[c]
            side[3 + c] = high[c]

    def lanes_of(row, index):
        return jnp.take_along_axis(
            jnp.broadcast_to(row, index.shape), index, axis=1, mode="promise_in_bounds"
        )

    def rim_force(k, c):
        start = k * lat
        place = lat_index + lax.rem(start, LANES)
        line = pl.ds(start // LANES, 1)
        turned = jnp.where(
            lane_index == 0,
            lanes_of(rim[c, line, :], place),
            jnp.where(lane_index == LANES - 1, lanes_of(rim[3 + c, line, :], place), 0.0),
        )
        edge = jnp.where(
            lat_index == 0,
            side[c, pl.ds(k, 1), :],
            jnp.where(lat_index == lat - 1, side[3 + c, pl.ds(k, 1), :], 0.0),
        )
        return turned + edge

    node_row = lax.broadcasted_iota(jnp.int16, (lat, LANES), 0)
    lane_16 = lax.broadcasted_iota(jnp.int16, (LANES, LANES), 0)
    facet_row = lax.broadcasted_iota(jnp.int16, (2 * n_rows, LANES), 0)
    facet_low = facet_row >= n_rows
    facet_row = jnp.where(facet_low, facet_row - jnp.int16(n_rows), facet_row)
    one = jnp.ones((LANES, LANES), jnp.bfloat16)
    none = jnp.zeros((LANES, LANES), jnp.bfloat16)
    slot_index = lax.broadcasted_iota(jnp.int32, (SUB, LANES), 0) * LANES + lax.broadcasted_iota(
        jnp.int32, (SUB, LANES), 1
    )

    def group_at(g):
        return pl.ds(pl.multiple_of(g * SUB, SUB), SUB)

    def look(lines, index):
        row, lane = index >> 7, index & (LANES - 1)
        found = None
        for i, line in enumerate(lines):
            here = [lanes_of(x, lane) for x in line]
            found = here if i == 0 else [jnp.where(row == i, x, y) for x, y in zip(here, found)]
        return found

    def pick(source, g):
        lines = [[source[c, rows - lat + i : rows - lat + i + 1, :] for c in range(3)] for i in range(lat)]
        return look(lines, nodes[group_at(g), :])

    def pick_facet(g):
        lines = [[table[a, i : i + 1, :] for a in range(4)] for i in range(n_rows)]
        return look(lines, slots[group_at(g), :])

    def press(g, u, h, sx, sy, ks):
        live = slot_index + g * (SUB * LANES) < count[0, 0]
        return jnp.where(live, ks * jnp.maximum(h + sx * u[0] + sy * u[1] - u[2], 0.0), 0.0)

    def wide(ref_row, height_of, dtype):
        return jnp.broadcast_to(ref_row, (height_of, LANES)).astype(dtype)

    def hot(ref, row):
        return jnp.where(lane_16 == wide(ref[pl.ds(row, 1), :] & (LANES - 1), LANES, jnp.int16), one, none)

    def scatter_force(step, g, pushed):
        at = group_at(g)
        normal = normals[step, at, :]
        values = (-facet_vals[1, at, :] * normal, -facet_vals[2, at, :] * normal, normal)
        high, low = zip(*[split_two(x) for x in values])
        for i, x in enumerate(high + low):
            parts[i, at, :] = x
        spread, hots = [], []
        for s in range(SUB):
            row = g * SUB + s
            mask = node_row == wide(nodes[pl.ds(row, 1), :] >> 7, lat, jnp.int16)
            spread.append(
                jnp.concatenate(
                    [
                        jnp.where(mask, wide(parts[i, pl.ds(row, 1), :], lat, jnp.bfloat16), none[:lat])
                        for i in range(6)
                    ],
                    axis=0,
                )
            )
            hots.append(hot(nodes, row))
        return pushed + lax.dot_general(
            jnp.concatenate(spread, axis=1), jnp.concatenate(hots, axis=1), NT, preferred_element_type=jnp.float32
        )

    def scatter_load(g, loads):
        at = group_at(g)
        high, low = split_two(normals[0, at, :] + normals[1, at, :])
        parts[6, at, :] = high
        parts[7, at, :] = low
        spread, hots = [], []
        for s in range(SUB):
            row = g * SUB + s
            mask = facet_row == wide(slots[pl.ds(row, 1), :] >> 7, 2 * n_rows, jnp.int16)
            both = jnp.where(
                facet_low,
                wide(parts[7, pl.ds(row, 1), :], 2 * n_rows, jnp.bfloat16),
                wide(parts[6, pl.ds(row, 1), :], 2 * n_rows, jnp.bfloat16),
            )
            spread.append(jnp.where(mask, both, jnp.zeros((2 * n_rows, LANES), jnp.bfloat16)))
            hots.append(hot(slots, row))
        return loads + lax.dot_general(
            jnp.concatenate(spread, axis=1), jnp.concatenate(hots, axis=1), NT, preferred_element_type=jnp.float32
        )

    no_push = jnp.zeros((6 * lat, LANES), jnp.float32)

    def add_outer(pushed):
        for c in range(3):
            here = pushed[c * lat : (c + 1) * lat] + pushed[(3 + c) * lat : (4 + c) * lat]
            force[c, rows - lat : rows, :] = force[c, rows - lat : rows, :] + here

    for copy in loads_in[2:5]:
        copy.wait()
    interior(disp)

    def pick_first(g, _):
        for c, x in enumerate(pick(disp, g)):
            picked[c, group_at(g), :] = x
        return 0

    lax.fori_loop(0, groups, pick_first, 0, unroll=2)

    def fill_scale(k, _):
        at = layer_rows(k)
        scale[at, :] = time_step / mass[at, :]
        return 0

    lax.fori_loop(0, layers, fill_scale, 0, unroll=2)

    for copy in loads_in[5:] + own_copies + facet_copies:
        copy.wait()
    for j in range(tiles_need):
        for i in range(half):
            row = tiles[0, j] * half + i
            for a in range(4):
                table[a, j * half + i : j * half + i + 1, :] = facet_all[
                    a * n_road + row // patch_rows, pl.ds(row % patch_rows, 1), :
                ]

    def first_press(g, _):
        at = group_at(g)
        values = pick_facet(g)
        for a in range(4):
            facet_vals[a, at, :] = values[a]
        normals[0, at, :] = press(g, [picked[c, at, :] for c in range(3)], *values)
        return 0

    lax.fori_loop(0, groups, first_press, 0, unroll=2)
    add_outer(lax.fori_loop(0, groups, functools.partial(scatter_force, 0), no_push, unroll=2))

    def advance(k, _):
        at = layer_rows(k)
        for c in range(3):
            v = veloc[c, at, :] + scale[at, :] * (force[c, at, :] + rim_force(k, c))
            v1[c, at, :] = v
            u1[c, at, :] = disp[c, at, :] + time_step * v
        return 0

    for copy in halos0:
        copy.wait()
    fill_rim(0)
    advance(layers - 1, 0)

    def second_press(g, _):
        at = group_at(g)
        normals[1, at, :] = press(g, pick(u1, g), *[facet_vals[a, at, :] for a in range(4)])
        return 0

    lax.fori_loop(0, groups, second_press, 0, unroll=2)
    loads = lax.fori_loop(0, groups, scatter_load, jnp.zeros((2 * n_rows, LANES), jnp.float32), unroll=2)
    loads = loads[:n_rows] + loads[n_rows:]

    if in_kernel_sum:
        loads_all[r] = loads
        road_copies = []
        for offset in range(1, n_road):
            copy = pltpu.make_async_remote_copy(
                src_ref=loads_all.at[r],
                dst_ref=loads_all.at[r],
                send_sem=road_sems.at[0, offset - 1],
                recv_sem=road_sems.at[1, offset - 1],
                device_id=road_peer(offset),
                device_id_type=MESH,
            )
            copy.start()
            road_copies.append(copy)
    else:
        row = lax.broadcasted_iota(jnp.int32, load_out.shape, 0)
        total = jnp.zeros(load_out.shape, jnp.float32)
        for j in range(n_rows):
            total = total + jnp.where(row == tiles[0, j // half] * half + j % half, loads[j : j + 1, :], 0.0)
        load_out[...] = total

    lax.fori_loop(0, layers - 1, advance, 0, unroll=3)
    fill_faces(1, u1)
    halos1 = halo_copies(1)
    for copy in halos1:
        copy.start()

    if in_kernel_sum:
        for copy in tile_copies + road_copies:
            copy.wait()
        chunk_rows = load_out.shape[0]
        row = lax.broadcasted_iota(jnp.int32, (n_blk * chunk_rows, LANES), 0)
        row = (row // chunk_rows * n_road + r) * chunk_rows + row % chunk_rows
        total = jnp.zeros((n_blk * chunk_rows, LANES), jnp.float32)
        for i in range(n_road):
            first_rows = tiles_all[i] * half
            for j in range(n_rows):
                here = first_rows[:, j // half : j // half + 1] + j % half
                total = total + jnp.where(row == here, loads_all[i, j : j + 1, :], 0.0)
        for i in range(n_blk):
            reduced[i] = total[i * chunk_rows : (i + 1) * chunk_rows]
        blk_copies = []
        for offset in range(1, n_blk):
            copy = pltpu.make_async_remote_copy(
                src_ref=reduced.at[lax.rem(b + offset, n_blk)],
                dst_ref=blk_recv.at[offset - 1],
                send_sem=blk_sems.at[0, offset - 1],
                recv_sem=blk_sems.at[1, offset - 1],
                device_id=blk_peer(offset),
                device_id_type=MESH,
            )
            copy.start()
            blk_copies.append(copy)

    interior(u1)
    add_outer(lax.fori_loop(0, groups, functools.partial(scatter_force, 1), no_push, unroll=2))
    for copy in halos1:
        copy.wait()
    fill_rim(1)

    def finish(k, _):
        at = layer_rows(k)
        for c in range(3):
            v_out[c, at, :] = v1[c, at, :] + scale[at, :] * (force[c, at, :] + rim_force(k, c))
        return 0

    lax.fori_loop(0, layers, finish, 0, unroll=2)

    if in_kernel_sum:
        for copy in blk_copies:
            copy.wait()
        total = reduced[b]
        for i in range(n_blk - 1):
            total = total + blk_recv[i]
        load_out[...] = total


def write_out(v_in, load_in, v_out, load_out, sems):
    copies = [
        pltpu.make_async_copy(src, dst, sems.at[i])
        for i, (src, dst) in enumerate(((v_in, v_out), (load_in, load_out)))
    ]
    for copy in copies:
        copy.start()
    for copy in copies:
        copy.wait()


def on_device(
    n_blk,
    n_road,
    disp,
    veloc,
    stiff,
    mass,
    road_height,
    road_slope_x,
    road_slope_y,
    road_stiff,
    tile_list,
    pair_node,
    pair_slot,
    pair_count,
):
    _, layers, lat, lanes = disp.shape
    rows = layers * lat
    pairs = pair_node.shape[-1]
    pair_rows = pairs // LANES
    tiles_need = tile_list.shape[-1]
    patch_rows = road_height.shape[0] // LANES
    total_rows = patch_rows * n_road
    table_rows = tiles_need * TILE // LANES
    devices = n_blk * n_road
    in_kernel_sum = total_rows % devices == 0
    f32 = jnp.float32
    if in_kernel_sum:
        load_shape = (total_rows // devices, LANES)
    else:
        load_shape = (total_rows, LANES)
    scratch = [
        pltpu.VMEM((3, rows, lanes), f32),
        pltpu.VMEM((3, rows, lanes), f32),
        pltpu.VMEM((3, rows, lanes), f32),
        pltpu.VMEM((rows, lanes), f32),
        pltpu.VMEM((pair_rows, LANES), jnp.int32),
        pltpu.VMEM((pair_rows, LANES), jnp.int32),
        pltpu.SMEM((1, tiles_need), jnp.int32),
        pltpu.SMEM((1, 1), jnp.int32),
        pltpu.SemaphoreType.DMA((8,)),
        pltpu.SemaphoreType.DMA((5,)),
        pltpu.VMEM((3, pair_rows, LANES), f32),
        pltpu.VMEM((4, pair_rows, LANES), f32),
        pltpu.VMEM((2, pair_rows, LANES), f32),
        pltpu.VMEM((8, pair_rows, LANES), f32),
        pltpu.VMEM((3, rows, lanes), f32),
        pltpu.VMEM((3, rows, lanes), f32),
        pltpu.VMEM((3, rows, lanes), f32),
        pltpu.VMEM((rows, lanes), f32),
        pltpu.VMEM((6, rows // LANES, LANES), f32),
        pltpu.VMEM((6, layers, lanes), f32),
        pltpu.VMEM((4 * n_road, patch_rows, LANES), f32),
        pltpu.VMEM((4, table_rows, LANES), f32),
        pltpu.VMEM((2, 3, rows), f32),
        pltpu.VMEM((2, 4, rows), f32),
        pltpu.VMEM((2, 3, rows), f32),
        pltpu.VMEM((2, 4, rows), f32),
        pltpu.VMEM((2, 3, layers, lanes), f32),
        pltpu.VMEM((2, 4, layers, lanes), f32),
        pltpu.VMEM((2, 3, layers, lanes), f32),
        pltpu.VMEM((2, 4, layers, lanes), f32),
        pltpu.SemaphoreType.DMA((2, 2, 4)),
        pltpu.SemaphoreType.DMA((2, 4, n_road - 1)),
    ]
    if in_kernel_sum:
        scratch += [
            pltpu.VMEM((n_road, 1, tiles_need), jnp.int32),
            pltpu.VMEM((n_road, table_rows, LANES), f32),
            pltpu.VMEM((n_blk,) + load_shape, f32),
            pltpu.VMEM((n_blk - 1,) + load_shape, f32),
            pltpu.SemaphoreType.DMA((2, n_road - 1)),
            pltpu.SemaphoreType.DMA((2, n_road - 1)),
            pltpu.SemaphoreType.DMA((2, n_blk - 1)),
        ]
    vmem = pl.BlockSpec(memory_space=pltpu.VMEM)
    hbm = pl.BlockSpec(memory_space=pltpu.HBM)
    anywhere = pl.BlockSpec(memory_space=pl.ANY)
    velocity, load = pl.pallas_call(
        functools.partial(kernel, n_blk, n_road, lat, in_kernel_sum),
        out_shape=(
            pltpu.VMEM((3, rows, lanes), f32),
            pltpu.VMEM(load_shape, f32),
        ),
        in_specs=[hbm] * 12,
        out_specs=(vmem, vmem),
        scratch_shapes=scratch,
        compiler_params=pltpu.CompilerParams(collective_id=0, has_side_effects=True),
    )(
        disp.reshape(3, rows, lanes),
        veloc.reshape(3, rows, lanes),
        stiff.reshape(3, rows, lanes),
        mass.reshape(rows, lanes),
        road_height.reshape(patch_rows, LANES),
        road_slope_x.reshape(patch_rows, LANES),
        road_slope_y.reshape(patch_rows, LANES),
        road_stiff.reshape(patch_rows, LANES),
        tile_list.reshape(1, tiles_need),
        pair_node.reshape(pair_rows, LANES),
        pair_slot.reshape(pair_rows, LANES),
        pair_count.reshape(1, 1),
    )
    velocity, load = pl.pallas_call(
        write_out,
        out_shape=(
            jax.ShapeDtypeStruct(velocity.shape, f32),
            jax.ShapeDtypeStruct(load.shape, f32),
        ),
        in_specs=[vmem] * 2,
        out_specs=(hbm, hbm),
        scratch_shapes=[pltpu.SemaphoreType.DMA((2,))],
    )(*(pltpu.with_memory_space_constraint(x, pltpu.VMEM) for x in (velocity, load)))
    load = load.reshape(-1)
    if not in_kernel_sum:
        load = lax.psum_scatter(load, ("blk", "road"), scatter_dimension=0, tiled=True)
    return velocity.reshape(disp.shape), load


def solution(mesh):
    in_specs = (
        P(None, None, "road", "blk"),
        P(None, None, "road", "blk"),
        P(None, None, "road", "blk"),
        P(None, "road", "blk"),
        P("road"),
        P("road"),
        P("road"),
        P("road"),
        P("blk", "road", None),
        P("blk", "road", None),
        P("blk", "road", None),
        P("blk", "road"),
    )
    out_specs = (P(None, None, "road", "blk"), P(("blk", "road")))
    body = functools.partial(on_device, mesh.shape["blk"], mesh.shape["road"])
    return jax.shard_map(body, mesh=mesh, in_specs=in_specs, out_specs=out_specs, check_vma=False)
```

```python
import functools

import jax
import jax.numpy as jnp
from jax import lax
from jax.experimental import pallas as pl
from jax.experimental.pallas import tpu as pltpu
from jax.sharding import PartitionSpec as P

TILE = 256
LANES = 128
SUB = 8

hardening = 0.5
time_step = 0.25

MESH = pl.DeviceIdType.MESH
NT = (((1,), (1,)), ((), ()))


def split_two(x):
    high = x.astype(jnp.bfloat16).astype(jnp.float32)
    return high, x - high


def tension(weights, strain):
    squared = strain[0] * strain[0] + strain[1] * strain[1] + strain[2] * strain[2]
    scaled = weights * (1.0 + hardening * squared)
    return [scaled * s for s in strain]


def kernel(
    n_blk,
    n_road,
    lat,
    in_kernel_sum,
    disp_in,
    veloc_in,
    stiff_in,
    mass_in,
    height,
    slope_x,
    slope_y,
    road_stiff,
    tiles_in,
    nodes_in,
    slots_in,
    count_in,
    v_out,
    load_out,
    disp,
    veloc,
    stiff,
    mass,
    nodes,
    slots,
    tiles,
    count,
    in_sems,
    own_sems,
    picked,
    facet_vals,
    normals,
    parts,
    u1,
    v1,
    force,
    scale,
    rim,
    side,
    facet_all,
    table,
    up_send,
    down_send,
    up_recv,
    down_recv,
    side_up_send,
    side_down_send,
    side_up_recv,
    side_down_recv,
    halo_sems,
    facet_sems,
    *reduction,
):
    b = lax.axis_index("blk")
    r = lax.axis_index("road")
    rows = disp.shape[1]
    layers = rows // lat
    groups = nodes.shape[0] // SUB
    n_rows = table.shape[1]
    tiles_need = tiles.shape[1]
    half = n_rows // tiles_need
    patch_rows = height.shape[0]

    def road_peer(offset):
        return {"blk": b, "road": lax.rem(r + offset, n_road)}

    def blk_peer(offset):
        return {"blk": lax.rem(b + offset, n_blk), "road": r}

    def blk_place(t):
        return {"blk": t, "road": r}

    def greet(t, _):
        pl.semaphore_signal(barrier, inc=1, device_id=blk_place(t), device_id_type=MESH)
        return 0

    barrier = pltpu.get_barrier_semaphore()
    for offset in range(1, n_road):
        pl.semaphore_signal(barrier, inc=1, device_id=road_peer(offset), device_id_type=MESH)
    if in_kernel_sum:
        lax.fori_loop(b - (b + n_blk - 1) // n_blk, b, greet, 0)
        lax.fori_loop(b + 1, n_blk, greet, 0)
        greeted = b + 1 - b // (n_blk - 1)
    else:
        for offset in sorted({1, n_blk - 1}):
            greet(lax.rem(b + offset, n_blk), 0)
        greeted = len({1, n_blk - 1})

    def fill_faces(step, source):
        for c in range(3):
            turned = source[c].T
            up_send[step, c : c + 1, :] = turned[LANES - 1 : LANES, :]
            down_send[step, c : c + 1, :] = turned[0:1, :]
            side_up_send[step, c] = source[c, pl.ds(lat - 1, layers, stride=lat), :]
            side_down_send[step, c] = source[c, pl.ds(0, layers, stride=lat), :]
        if step == 0:
            down_send[step, 3:4, :] = stiff[2].T[0:1, :]
            side_down_send[step, 3] = stiff[1, pl.ds(0, layers, stride=lat), :]

    def halo_copies(step):
        plan = (
            (up_send, up_recv, blk_peer(1)),
            (down_send, down_recv, blk_peer(n_blk - 1)),
            (side_up_send, side_up_recv, road_peer(1)),
            (side_down_send, side_down_recv, road_peer(n_road - 1)),
        )
        return [
            pltpu.make_async_remote_copy(
                src_ref=src.at[step],
                dst_ref=dst.at[step],
                send_sem=halo_sems.at[step, 0, i],
                recv_sem=halo_sems.at[step, 1, i],
                device_id=peer,
                device_id_type=MESH,
            )
            for i, (src, dst, peer) in enumerate(plan)
        ]

    loads_in = [
        pltpu.make_async_copy(src, dst, in_sems.at[i])
        for i, (src, dst) in enumerate(
            (
                (disp_in, disp),
                (stiff_in, stiff),
                (nodes_in, nodes),
                (mass_in, mass),
                (veloc_in, veloc),
                (slots_in, slots),
                (tiles_in, tiles),
                (count_in, count),
            )
        )
    ]
    for copy in loads_in:
        copy.start()
    own = (height, slope_x, slope_y, road_stiff)
    own_copies = [
        pltpu.make_async_copy(own[a], facet_all.at[a * n_road + r], own_sems.at[a]) for a in range(4)
    ]
    if in_kernel_sum:
        tiles_all, loads_all, reduced, blk_recv, tile_sems, road_sems, blk_sems, late_sem = reduction
        own_copies.append(pltpu.make_async_copy(tiles_in, tiles_all.at[r], own_sems.at[4]))
    for copy in own_copies:
        copy.start()
    pl.semaphore_wait(barrier, greeted + n_road - 1)
    if in_kernel_sum:

        def tell(t, _):
            pl.semaphore_signal(late_sem, inc=1, device_id=blk_place(t), device_id_type=MESH)
            return 0

        lax.fori_loop(0, b, tell, 0)

    facet_copies = []
    for a in range(4):
        for offset in range(1, n_road):
            copy = pltpu.make_async_remote_copy(
                src_ref=own[a],
                dst_ref=facet_all.at[a * n_road + r],
                send_sem=facet_sems.at[0, a, offset - 1],
                recv_sem=facet_sems.at[1, a, offset - 1],
                device_id=road_peer(offset),
                device_id_type=MESH,
            )
            copy.start()
            facet_copies.append(copy)
    for copy in loads_in[:2]:
        copy.wait()
    fill_faces(0, disp)
    halos0 = halo_copies(0)
    for i in (0, 2, 3):
        halos0[i].start()
    tile_copies = []
    if in_kernel_sum:
        for offset in range(1, n_road):
            copy = pltpu.make_async_remote_copy(
                src_ref=tiles_in,
                dst_ref=tiles_all.at[r],
                send_sem=tile_sems.at[0, offset - 1],
                recv_sem=tile_sems.at[1, offset - 1],
                device_id=road_peer(offset),
                device_id_type=MESH,
            )
            copy.start()
            tile_copies.append(copy)

    lat_index = lax.broadcasted_iota(jnp.int32, (lat, LANES), 0)
    lane_index = lax.broadcasted_iota(jnp.int32, (lat, LANES), 1)

    def layer_rows(k):
        return pl.ds(pl.multiple_of(k * lat, lat), lat)

    def inside(source, k, above, bottom):
        at = layer_rows(k)
        u = [source[c, at, :] for c in range(3)]
        if bottom:
            strain = u
        else:
            below = layer_rows(k - 1)
            strain = [u[c] - source[c, below, :] for c in range(3)]
        radial = tension(stiff[0, at, :], strain)
        beside = tension(stiff[1, at, :], [x - pltpu.roll(x, 1, 0) for x in u])
        around = tension(stiff[2, at, :], [x - pltpu.roll(x, 1, 1) for x in u])
        for c in range(3):
            t = jnp.where(lat_index == 0, 0.0, beside[c])
            w = jnp.where(lane_index == 0, 0.0, around[c])
            force[c, at, :] = (
                (above[c] - radial[c])
                + (pltpu.roll(t, lat - 1, 0) - t)
                + (pltpu.roll(w, LANES - 1, 1) - w)
            )
        return radial

    def interior(source):
        nothing = tuple(jnp.zeros((lat, LANES), jnp.float32) for _ in range(3))

        def body(i, above):
            return tuple(inside(source, layers - 1 - i, above, False))

        above = lax.fori_loop(0, layers - 1, body, nothing, unroll=5)
        inside(source, 0, above, True)

    def fill_rim(step):
        stiff_around = down_recv[0, 3:4, :]
        own_around = down_send[0, 3:4, :]
        low = tension(own_around, [down_send[step, c : c + 1, :] - up_recv[step, c : c + 1, :] for c in range(3)])
        high = tension(stiff_around, [down_recv[step, c : c + 1, :] - up_send[step, c : c + 1, :] for c in range(3)])
        for c in range(3):
            for i in range(rows // LANES):
                piece = slice(i * LANES, (i + 1) * LANES)
                rim[c, i : i + 1, :] = -low[c][:, piece]
                rim[3 + c, i : i + 1, :] = high[c][:, piece]
        first = jnp.where(r == 0, 0.0, 1.0)
        last = jnp.where(r == n_road - 1, 0.0, 1.0)
        low = tension(
            side_down_send[0, 3], [side_down_send[step, c] - first * side_up_recv[step, c] for c in range(3)]
        )
        high = tension(
            last * side_down_recv[0, 3], [side_down_recv[step, c] - side_up_send[step, c] for c in range(3)]
        )
        for c in range(3):
            side[c] = -low[c]
            side[3 + c] = high[c]

    def lanes_of(row, index):
        return jnp.take_along_axis(
            jnp.broadcast_to(row, index.shape), index, axis=1, mode="promise_in_bounds"
        )

    def rim_force(k, c):
        start = k * lat
        place = lat_index + lax.rem(start, LANES)
        line = pl.ds(start // LANES, 1)
        turned = jnp.where(
            lane_index == 0,
            lanes_of(rim[c, line, :], place),
            jnp.where(lane_index == LANES - 1, lanes_of(rim[3 + c, line, :], place), 0.0),
        )
        edge = jnp.where(
            lat_index == 0,
            side[c, pl.ds(k, 1), :],
            jnp.where(lat_index == lat - 1, side[3 + c, pl.ds(k, 1), :], 0.0),
        )
        return turned + edge

    node_row = lax.broadcasted_iota(jnp.int16, (lat, LANES), 0)
    lane_16 = lax.broadcasted_iota(jnp.int16, (LANES, LANES), 0)
    facet_row = lax.broadcasted_iota(jnp.int16, (2 * n_rows, LANES), 0)
    facet_low = facet_row >= n_rows
    facet_row = jnp.where(facet_low, facet_row - jnp.int16(n_rows), facet_row)
    one = jnp.ones((LANES, LANES), jnp.bfloat16)
    none = jnp.zeros((LANES, LANES), jnp.bfloat16)
    slot_index = lax.broadcasted_iota(jnp.int32, (SUB, LANES), 0) * LANES + lax.broadcasted_iota(
        jnp.int32, (SUB, LANES), 1
    )

    def group_at(g):
        return pl.ds(pl.multiple_of(g * SUB, SUB), SUB)

    def look(lines, index):
        row, lane = index >> 7, index & (LANES - 1)
        found = None
        for i, line in enumerate(lines):
            here = [lanes_of(x, lane) for x in line]
            found = here if i == 0 else [jnp.where(row == i, x, y) for x, y in zip(here, found)]
        return found

    def pick(source, g):
        lines = [[source[c, rows - lat + i : rows - lat + i + 1, :] for c in range(3)] for i in range(lat)]
        return look(lines, nodes[group_at(g), :])

    def pick_facet(g):
        lines = [[table[a, i : i + 1, :] for a in range(4)] for i in range(n_rows)]
        return look(lines, slots[group_at(g), :])

    def press(g, u, h, sx, sy, ks):
        live = slot_index + g * (SUB * LANES) < count[0]
        return jnp.where(live, ks * jnp.maximum(h + sx * u[0] + sy * u[1] - u[2], 0.0), 0.0)

    def wide(ref_row, height_of, dtype):
        return jnp.broadcast_to(ref_row, (height_of, LANES)).astype(dtype)

    def hot(ref, row):
        return jnp.where(lane_16 == wide(ref[pl.ds(row, 1), :] & (LANES - 1), LANES, jnp.int16), one, none)

    def scatter_force(step, g, pushed):
        at = group_at(g)
        normal = normals[step, at, :]
        values = (-facet_vals[1, at, :] * normal, -facet_vals[2, at, :] * normal, normal)
        high, low = zip(*[split_two(x) for x in values])
        for i, x in enumerate(high + low):
            parts[i, at, :] = x
        spread, hots = [], []
        for s in range(SUB):
            row = g * SUB + s
            mask = node_row == wide(nodes[pl.ds(row, 1), :] >> 7, lat, jnp.int16)
            spread.append(
                jnp.concatenate(
                    [
                        jnp.where(mask, wide(parts[i, pl.ds(row, 1), :], lat, jnp.bfloat16), none[:lat])
                        for i in range(6)
                    ],
                    axis=0,
                )
            )
            hots.append(hot(nodes, row))
        return pushed + lax.dot_general(
            jnp.concatenate(spread, axis=1), jnp.concatenate(hots, axis=1), NT, preferred_element_type=jnp.float32
        )

    def scatter_load(g, loads):
        at = group_at(g)
        high, low = split_two(normals[0, at, :] + normals[1, at, :])
        parts[6, at, :] = high
        parts[7, at, :] = low
        spread, hots = [], []
        for s in range(SUB):
            row = g * SUB + s
            mask = facet_row == wide(slots[pl.ds(row, 1), :] >> 7, 2 * n_rows, jnp.int16)
            both = jnp.where(
                facet_low,
                wide(parts[7, pl.ds(row, 1), :], 2 * n_rows, jnp.bfloat16),
                wide(parts[6, pl.ds(row, 1), :], 2 * n_rows, jnp.bfloat16),
            )
            spread.append(jnp.where(mask, both, jnp.zeros((2 * n_rows, LANES), jnp.bfloat16)))
            hots.append(hot(slots, row))
        return loads + lax.dot_general(
            jnp.concatenate(spread, axis=1), jnp.concatenate(hots, axis=1), NT, preferred_element_type=jnp.float32
        )

    no_push = jnp.zeros((6 * lat, LANES), jnp.float32)

    def add_outer(pushed):
        for c in range(3):
            here = pushed[c * lat : (c + 1) * lat] + pushed[(3 + c) * lat : (4 + c) * lat]
            force[c, rows - lat : rows, :] = force[c, rows - lat : rows, :] + here

    for copy in loads_in[2:5]:
        copy.wait()
    interior(disp)

    def pick_first(g, _):
        for c, x in enumerate(pick(disp, g)):
            picked[c, group_at(g), :] = x
        return 0

    lax.fori_loop(0, groups, pick_first, 0, unroll=8)

    def fill_scale(k, _):
        at = layer_rows(k)
        scale[at, :] = time_step / mass[at, :]
        return 0

    lax.fori_loop(0, layers, fill_scale, 0, unroll=8)

    if in_kernel_sum:

        @pl.when(b < n_blk - 1)
        def _():
            pl.semaphore_wait(late_sem, n_blk - 1 - b)

    halos0[1].start()
    for copy in loads_in[5:] + own_copies + facet_copies:
        copy.wait()
    for j in range(tiles_need):
        for i in range(half):
            row = tiles[0, j] * half + i
            for a in range(4):
                table[a, j * half + i : j * half + i + 1, :] = facet_all[
                    a * n_road + row // patch_rows, pl.ds(row % patch_rows, 1), :
                ]

    def first_press(g, _):
        at = group_at(g)
        values = pick_facet(g)
        for a in range(4):
            facet_vals[a, at, :] = values[a]
        normals[0, at, :] = press(g, [picked[c, at, :] for c in range(3)], *values)
        return 0

    lax.fori_loop(0, groups, first_press, 0, unroll=8)
    add_outer(lax.fori_loop(0, groups, functools.partial(scatter_force, 0), no_push, unroll=8))

    def advance(k, _):
        at = layer_rows(k)
        for c in range(3):
            v = veloc[c, at, :] + scale[at, :] * (force[c, at, :] + rim_force(k, c))
            v1[c, at, :] = v
            u1[c, at, :] = disp[c, at, :] + time_step * v
        return 0

    for copy in halos0:
        copy.wait()
    fill_rim(0)
    advance(layers - 1, 0)

    def second_press(g, _):
        at = group_at(g)
        normals[1, at, :] = press(g, pick(u1, g), *[facet_vals[a, at, :] for a in range(4)])
        return 0

    lax.fori_loop(0, groups, second_press, 0, unroll=8)
    loads = lax.fori_loop(0, groups, scatter_load, jnp.zeros((2 * n_rows, LANES), jnp.float32), unroll=8)
    loads = loads[:n_rows] + loads[n_rows:]

    if in_kernel_sum:
        loads_all[r] = loads
        road_copies = []
        for offset in range(1, n_road):
            copy = pltpu.make_async_remote_copy(
                src_ref=loads_all.at[r],
                dst_ref=loads_all.at[r],
                send_sem=road_sems.at[0, offset - 1],
                recv_sem=road_sems.at[1, offset - 1],
                device_id=road_peer(offset),
                device_id_type=MESH,
            )
            copy.start()
            road_copies.append(copy)
    else:
        row = lax.broadcasted_iota(jnp.int32, load_out.shape, 0)
        total = jnp.zeros(load_out.shape, jnp.float32)
        for j in range(n_rows):
            total = total + jnp.where(row == tiles[0, j // half] * half + j % half, loads[j : j + 1, :], 0.0)
        load_out[...] = total

    lax.fori_loop(0, layers - 1, advance, 0, unroll=5)
    fill_faces(1, u1)
    halos1 = halo_copies(1)
    for copy in halos1:
        copy.start()

    if in_kernel_sum:
        for copy in tile_copies + road_copies:
            copy.wait()
        chunk_rows = load_out.shape[0]
        row = lax.broadcasted_iota(jnp.int32, (n_blk * chunk_rows, LANES), 0)
        row = (row // chunk_rows * n_road + r) * chunk_rows + row % chunk_rows
        total = jnp.zeros((n_blk * chunk_rows, LANES), jnp.float32)
        for i in range(n_road):
            first_rows = tiles_all[i] * half
            for j in range(n_rows):
                here = first_rows[:, j // half : j // half + 1] + j % half
                total = total + jnp.where(row == here, loads_all[i, j : j + 1, :], 0.0)
        for i in range(n_blk):
            reduced[i] = total[i * chunk_rows : (i + 1) * chunk_rows]
        blk_copies = []
        for offset in range(1, n_blk):
            copy = pltpu.make_async_remote_copy(
                src_ref=reduced.at[lax.rem(b + offset, n_blk)],
                dst_ref=blk_recv.at[offset - 1],
                send_sem=blk_sems.at[0, offset - 1],
                recv_sem=blk_sems.at[1, offset - 1],
                device_id=blk_peer(offset),
                device_id_type=MESH,
            )
            copy.start()
            blk_copies.append(copy)

    interior(u1)
    add_outer(lax.fori_loop(0, groups, functools.partial(scatter_force, 1), no_push, unroll=8))
    for copy in halos1:
        copy.wait()
    fill_rim(1)

    def finish(k, _):
        at = layer_rows(k)
        for c in range(3):
            v_out[c, at, :] = v1[c, at, :] + scale[at, :] * (force[c, at, :] + rim_force(k, c))
        return 0

    lax.fori_loop(0, layers, finish, 0, unroll=8)

    if in_kernel_sum:
        for copy in blk_copies:
            copy.wait()
        total = reduced[b]
        for i in range(n_blk - 1):
            total = total + blk_recv[i]
        load_out[...] = total


def write_out(v_in, load_in, v_out, load_out, sems):
    copies = [
        pltpu.make_async_copy(src, dst, sems.at[i])
        for i, (src, dst) in enumerate(((v_in, v_out), (load_in, load_out)))
    ]
    for copy in copies:
        copy.start()
    for copy in copies:
        copy.wait()


def on_device(
    n_blk,
    n_road,
    disp,
    veloc,
    stiff,
    mass,
    road_height,
    road_slope_x,
    road_slope_y,
    road_stiff,
    tile_list,
    pair_node,
    pair_slot,
    pair_count,
):
    _, layers, lat, lanes = disp.shape
    rows = layers * lat
    pairs = pair_node.shape[-1]
    pair_rows = pairs // LANES
    tiles_need = tile_list.shape[-1]
    patch_rows = road_height.shape[0] // LANES
    total_rows = patch_rows * n_road
    table_rows = tiles_need * TILE // LANES
    devices = n_blk * n_road
    in_kernel_sum = total_rows % devices == 0
    f32 = jnp.float32
    if in_kernel_sum:
        load_shape = (total_rows // devices, LANES)
    else:
        load_shape = (total_rows, LANES)
    scratch = [
        pltpu.VMEM((3, rows, lanes), f32),
        pltpu.VMEM((3, rows, lanes), f32),
        pltpu.VMEM((3, rows, lanes), f32),
        pltpu.VMEM((rows, lanes), f32),
        pltpu.VMEM((pair_rows, LANES), jnp.int32),
        pltpu.VMEM((pair_rows, LANES), jnp.int32),
        pltpu.SMEM((1, tiles_need), jnp.int32),
        pltpu.SMEM((1,), jnp.int32),
        pltpu.SemaphoreType.DMA((8,)),
        pltpu.SemaphoreType.DMA((5,)),
        pltpu.VMEM((3, pair_rows, LANES), f32),
        pltpu.VMEM((4, pair_rows, LANES), f32),
        pltpu.VMEM((2, pair_rows, LANES), f32),
        pltpu.VMEM((8, pair_rows, LANES), f32),
        pltpu.VMEM((3, rows, lanes), f32),
        pltpu.VMEM((3, rows, lanes), f32),
        pltpu.VMEM((3, rows, lanes), f32),
        pltpu.VMEM((rows, lanes), f32),
        pltpu.VMEM((6, rows // LANES, LANES), f32),
        pltpu.VMEM((6, layers, lanes), f32),
        pltpu.VMEM((4 * n_road, patch_rows, LANES), f32),
        pltpu.VMEM((4, table_rows, LANES), f32),
        pltpu.VMEM((2, 3, rows), f32),
        pltpu.VMEM((2, 4, rows), f32),
        pltpu.VMEM((2, 3, rows), f32),
        pltpu.VMEM((2, 4, rows), f32),
        pltpu.VMEM((2, 3, layers, lanes), f32),
        pltpu.VMEM((2, 4, layers, lanes), f32),
        pltpu.VMEM((2, 3, layers, lanes), f32),
        pltpu.VMEM((2, 4, layers, lanes), f32),
        pltpu.SemaphoreType.DMA((2, 2, 4)),
        pltpu.SemaphoreType.DMA((2, 4, n_road - 1)),
    ]
    if in_kernel_sum:
        scratch += [
            pltpu.VMEM((n_road, 1, tiles_need), jnp.int32),
            pltpu.VMEM((n_road, table_rows, LANES), f32),
            pltpu.VMEM((n_blk,) + load_shape, f32),
            pltpu.VMEM((n_blk - 1,) + load_shape, f32),
            pltpu.SemaphoreType.DMA((2, n_road - 1)),
            pltpu.SemaphoreType.DMA((2, n_road - 1)),
            pltpu.SemaphoreType.DMA((2, n_blk - 1)),
            pltpu.SemaphoreType.REGULAR,
        ]
    vmem = pl.BlockSpec(memory_space=pltpu.VMEM)
    hbm = pl.BlockSpec(memory_space=pltpu.HBM)
    anywhere = pl.BlockSpec(memory_space=pl.ANY)
    velocity, load = pl.pallas_call(
        functools.partial(kernel, n_blk, n_road, lat, in_kernel_sum),
        out_shape=(
            pltpu.VMEM((3, rows, lanes), f32),
            pltpu.VMEM(load_shape, f32),
        ),
        in_specs=[hbm] * 12,
        out_specs=(vmem, vmem),
        scratch_shapes=scratch,
        compiler_params=pltpu.CompilerParams(collective_id=0, has_side_effects=True),
    )(
        disp.reshape(3, rows, lanes),
        veloc.reshape(3, rows, lanes),
        stiff.reshape(3, rows, lanes),
        mass.reshape(rows, lanes),
        road_height.reshape(patch_rows, LANES),
        road_slope_x.reshape(patch_rows, LANES),
        road_slope_y.reshape(patch_rows, LANES),
        road_stiff.reshape(patch_rows, LANES),
        tile_list.reshape(1, tiles_need),
        pair_node.reshape(pair_rows, LANES),
        pair_slot.reshape(pair_rows, LANES),
        pair_count.reshape(1,),
    )
    velocity, load = pl.pallas_call(
        write_out,
        out_shape=(
            jax.ShapeDtypeStruct(velocity.shape, f32),
            jax.ShapeDtypeStruct(load.shape, f32),
        ),
        in_specs=[vmem] * 2,
        out_specs=(hbm, hbm),
        scratch_shapes=[pltpu.SemaphoreType.DMA((2,))],
    )(*(pltpu.with_memory_space_constraint(x, pltpu.VMEM) for x in (velocity, load)))
    load = load.reshape(-1)
    if not in_kernel_sum:
        load = lax.psum_scatter(load, ("blk", "road"), scatter_dimension=0, tiled=True)
    return velocity.reshape(disp.shape), load


def solution(mesh):
    in_specs = (
        P(None, None, "road", "blk"),
        P(None, None, "road", "blk"),
        P(None, None, "road", "blk"),
        P(None, "road", "blk"),
        P("road"),
        P("road"),
        P("road"),
        P("road"),
        P("blk", "road", None),
        P("blk", "road", None),
        P("blk", "road", None),
        P("blk", "road"),
    )
    out_specs = (P(None, None, "road", "blk"), P(("blk", "road")))
    body = functools.partial(on_device, mesh.shape["blk"], mesh.shape["road"])
    return jax.shard_map(body, mesh=mesh, in_specs=in_specs, out_specs=out_specs, check_vma=False)
```

```python
import functools

import jax
import jax.numpy as jnp
from jax import lax
from jax.experimental import pallas as pl
from jax.experimental.pallas import tpu as pltpu
from jax.sharding import PartitionSpec as P

TILE = 256
LANES = 128
SUB = 8

hardening = 0.5
time_step = 0.25

MESH = pl.DeviceIdType.MESH
NT = (((1,), (1,)), ((), ()))


def split_two(x):
    high = x.astype(jnp.bfloat16).astype(jnp.float32)
    return high, x - high


def tension(weights, strain):
    squared = strain[0] * strain[0] + strain[1] * strain[1] + strain[2] * strain[2]
    scaled = weights * (1.0 + hardening * squared)
    return [scaled * s for s in strain]


def kernel(
    n_blk,
    n_road,
    lat,
    in_kernel_sum,
    disp_in,
    veloc_in,
    stiff_in,
    mass_in,
    height,
    slope_x,
    slope_y,
    road_stiff,
    tiles_in,
    nodes_in,
    slots_in,
    count_in,
    v_out,
    load_out,
    disp,
    veloc,
    stiff,
    mass,
    nodes,
    slots,
    tiles,
    count,
    in_sems,
    own_sems,
    picked,
    facet_vals,
    normals,
    parts,
    u1,
    v1,
    force,
    scale,
    rim,
    side,
    facet_all,
    table,
    up_send,
    down_send,
    up_recv,
    down_recv,
    side_up_send,
    side_down_send,
    side_up_recv,
    side_down_recv,
    halo_sems,
    facet_sems,
    *reduction,
):
    b = lax.axis_index("blk")
    r = lax.axis_index("road")
    rows = disp.shape[1]
    layers = rows // lat
    groups = nodes.shape[0] // SUB
    n_rows = table.shape[1]
    tiles_need = tiles.shape[1]
    half = n_rows // tiles_need
    patch_rows = height.shape[0]

    def road_peer(offset):
        return {"blk": b, "road": lax.rem(r + offset, n_road)}

    def blk_peer(offset):
        return {"blk": lax.rem(b + offset, n_blk), "road": r}

    def blk_place(t):
        return {"blk": t, "road": r}

    def greet(t, _):
        pl.semaphore_signal(barrier, inc=1, device_id=blk_place(t), device_id_type=MESH)
        return 0

    def place(t, offset):
        return {"blk": t, "road": lax.rem(r + offset, n_road)}

    def notify(sem, offset, t, _):
        pl.semaphore_signal(sem, inc=1, device_id=place(t, offset), device_id_type=MESH)
        return 0

    barrier = pltpu.get_barrier_semaphore()
    for offset in range(1, n_road):
        pl.semaphore_signal(barrier, inc=1, device_id=road_peer(offset), device_id_type=MESH)
    if in_kernel_sum:
        lax.fori_loop(b - (b + n_blk - 1) // n_blk, b, greet, 0)
        for offset in range(n_road):
            lax.fori_loop(b + 1, n_blk, functools.partial(notify, barrier, offset), 0)
        greeted = b * n_road + 1 - b // (n_blk - 1)
    else:
        for offset in sorted({1, n_blk - 1}):
            greet(lax.rem(b + offset, n_blk), 0)
        greeted = len({1, n_blk - 1})

    def fill_faces(step, source):
        for c in range(3):
            turned = source[c].T
            up_send[step, c : c + 1, :] = turned[LANES - 1 : LANES, :]
            down_send[step, c : c + 1, :] = turned[0:1, :]
            side_up_send[step, c] = source[c, pl.ds(lat - 1, layers, stride=lat), :]
            side_down_send[step, c] = source[c, pl.ds(0, layers, stride=lat), :]
        if step == 0:
            down_send[step, 3:4, :] = stiff[2].T[0:1, :]
            side_down_send[step, 3] = stiff[1, pl.ds(0, layers, stride=lat), :]

    def halo_copies(step):
        plan = (
            (up_send, up_recv, blk_peer(1)),
            (down_send, down_recv, blk_peer(n_blk - 1)),
            (side_up_send, side_up_recv, road_peer(1)),
            (side_down_send, side_down_recv, road_peer(n_road - 1)),
        )
        return [
            pltpu.make_async_remote_copy(
                src_ref=src.at[step],
                dst_ref=dst.at[step],
                send_sem=halo_sems.at[step, 0, i],
                recv_sem=halo_sems.at[step, 1, i],
                device_id=peer,
                device_id_type=MESH,
            )
            for i, (src, dst, peer) in enumerate(plan)
        ]

    loads_in = [
        pltpu.make_async_copy(src, dst, in_sems.at[i])
        for i, (src, dst) in enumerate(
            (
                (disp_in, disp),
                (stiff_in, stiff),
                (nodes_in, nodes),
                (mass_in, mass),
                (veloc_in, veloc),
                (slots_in, slots),
                (tiles_in, tiles),
                (count_in, count),
            )
        )
    ]
    for copy in loads_in:
        copy.start()
    own = (height, slope_x, slope_y, road_stiff)
    own_copies = [
        pltpu.make_async_copy(own[a], facet_all.at[a * n_road + r], own_sems.at[a]) for a in range(4)
    ]
    if in_kernel_sum:
        spread_out, spread_recv, spread_sems, late_sem, far_sem = reduction
    for copy in own_copies:
        copy.start()
    pl.semaphore_wait(barrier, greeted + n_road - 1)
    if in_kernel_sum:
        for offset in range(n_road):
            lax.fori_loop(0, b, functools.partial(notify, far_sem if offset else late_sem, offset), 0)

    facet_copies = []
    for a in range(4):
        for offset in range(1, n_road):
            copy = pltpu.make_async_remote_copy(
                src_ref=own[a],
                dst_ref=facet_all.at[a * n_road + r],
                send_sem=facet_sems.at[0, a, offset - 1],
                recv_sem=facet_sems.at[1, a, offset - 1],
                device_id=road_peer(offset),
                device_id_type=MESH,
            )
            copy.start()
            facet_copies.append(copy)
    for copy in loads_in[:2]:
        copy.wait()
    fill_faces(0, disp)
    halos0 = halo_copies(0)
    for i in (0, 2, 3):
        halos0[i].start()
    if in_kernel_sum:

        @pl.when(b < n_blk - 1)
        def _():
            pl.semaphore_wait(late_sem, n_blk - 1 - b)

    halos0[1].start()

    lat_index = lax.broadcasted_iota(jnp.int32, (lat, LANES), 0)
    lane_index = lax.broadcasted_iota(jnp.int32, (lat, LANES), 1)

    def layer_rows(k):
        return pl.ds(pl.multiple_of(k * lat, lat), lat)

    def inside(source, k, above, bottom):
        at = layer_rows(k)
        u = [source[c, at, :] for c in range(3)]
        if bottom:
            strain = u
        else:
            below = layer_rows(k - 1)
            strain = [u[c] - source[c, below, :] for c in range(3)]
        radial = tension(stiff[0, at, :], strain)
        beside = tension(stiff[1, at, :], [x - pltpu.roll(x, 1, 0) for x in u])
        around = tension(stiff[2, at, :], [x - pltpu.roll(x, 1, 1) for x in u])
        for c in range(3):
            t = jnp.where(lat_index == 0, 0.0, beside[c])
            w = jnp.where(lane_index == 0, 0.0, around[c])
            force[c, at, :] = (
                (above[c] - radial[c])
                + (pltpu.roll(t, lat - 1, 0) - t)
                + (pltpu.roll(w, LANES - 1, 1) - w)
            )
        return radial

    def interior(source):
        nothing = tuple(jnp.zeros((lat, LANES), jnp.float32) for _ in range(3))

        def body(i, above):
            return tuple(inside(source, layers - 1 - i, above, False))

        above = lax.fori_loop(0, layers - 1, body, nothing, unroll=5)
        inside(source, 0, above, True)

    def fill_rim(step):
        stiff_around = down_recv[0, 3:4, :]
        own_around = down_send[0, 3:4, :]
        low = tension(own_around, [down_send[step, c : c + 1, :] - up_recv[step, c : c + 1, :] for c in range(3)])
        high = tension(stiff_around, [down_recv[step, c : c + 1, :] - up_send[step, c : c + 1, :] for c in range(3)])
        for c in range(3):
            for i in range(rows // LANES):
                piece = slice(i * LANES, (i + 1) * LANES)
                rim[c, i : i + 1, :] = -low[c][:, piece]
                rim[3 + c, i : i + 1, :] = high[c][:, piece]
        first = jnp.where(r == 0, 0.0, 1.0)
        last = jnp.where(r == n_road - 1, 0.0, 1.0)
        low = tension(
            side_down_send[0, 3], [side_down_send[step, c] - first * side_up_recv[step, c] for c in range(3)]
        )
        high = tension(
            last * side_down_recv[0, 3], [side_down_recv[step, c] - side_up_send[step, c] for c in range(3)]
        )
        for c in range(3):
            side[c] = -low[c]
            side[3 + c] = high[c]

    def lanes_of(row, index):
        return jnp.take_along_axis(
            jnp.broadcast_to(row, index.shape), index, axis=1, mode="promise_in_bounds"
        )

    def rim_force(k, c):
        start = k * lat
        place = lat_index + lax.rem(start, LANES)
        line = pl.ds(start // LANES, 1)
        turned = jnp.where(
            lane_index == 0,
            lanes_of(rim[c, line, :], place),
            jnp.where(lane_index == LANES - 1, lanes_of(rim[3 + c, line, :], place), 0.0),
        )
        edge = jnp.where(
            lat_index == 0,
            side[c, pl.ds(k, 1), :],
            jnp.where(lat_index == lat - 1, side[3 + c, pl.ds(k, 1), :], 0.0),
        )
        return turned + edge

    node_row = lax.broadcasted_iota(jnp.int16, (lat, LANES), 0)
    lane_16 = lax.broadcasted_iota(jnp.int16, (LANES, LANES), 0)
    facet_row = lax.broadcasted_iota(jnp.int16, (2 * n_rows, LANES), 0)
    facet_low = facet_row >= n_rows
    facet_row = jnp.where(facet_low, facet_row - jnp.int16(n_rows), facet_row)
    one = jnp.ones((LANES, LANES), jnp.bfloat16)
    none = jnp.zeros((LANES, LANES), jnp.bfloat16)
    slot_index = lax.broadcasted_iota(jnp.int32, (SUB, LANES), 0) * LANES + lax.broadcasted_iota(
        jnp.int32, (SUB, LANES), 1
    )

    def group_at(g):
        return pl.ds(pl.multiple_of(g * SUB, SUB), SUB)

    def look(lines, index):
        row, lane = index >> 7, index & (LANES - 1)
        found = None
        for i, line in enumerate(lines):
            here = [lanes_of(x, lane) for x in line]
            found = here if i == 0 else [jnp.where(row == i, x, y) for x, y in zip(here, found)]
        return found

    def pick(source, g):
        lines = [[source[c, rows - lat + i : rows - lat + i + 1, :] for c in range(3)] for i in range(lat)]
        return look(lines, nodes[group_at(g), :])

    def pick_facet(g):
        lines = [[table[a, i : i + 1, :] for a in range(4)] for i in range(n_rows)]
        return look(lines, slots[group_at(g), :])

    def press(g, u, h, sx, sy, ks):
        live = slot_index + g * (SUB * LANES) < count[0]
        return jnp.where(live, ks * jnp.maximum(h + sx * u[0] + sy * u[1] - u[2], 0.0), 0.0)

    def wide(ref_row, height_of, dtype):
        return jnp.broadcast_to(ref_row, (height_of, LANES)).astype(dtype)

    def hot(ref, row):
        return jnp.where(lane_16 == wide(ref[pl.ds(row, 1), :] & (LANES - 1), LANES, jnp.int16), one, none)

    def scatter_force(step, g, pushed):
        at = group_at(g)
        normal = normals[step, at, :]
        values = (-facet_vals[1, at, :] * normal, -facet_vals[2, at, :] * normal, normal)
        high, low = zip(*[split_two(x) for x in values])
        for i, x in enumerate(high + low):
            parts[i, at, :] = x
        spread, hots = [], []
        for s in range(SUB):
            row = g * SUB + s
            mask = node_row == wide(nodes[pl.ds(row, 1), :] >> 7, lat, jnp.int16)
            spread.append(
                jnp.concatenate(
                    [
                        jnp.where(mask, wide(parts[i, pl.ds(row, 1), :], lat, jnp.bfloat16), none[:lat])
                        for i in range(6)
                    ],
                    axis=0,
                )
            )
            hots.append(hot(nodes, row))
        return pushed + lax.dot_general(
            jnp.concatenate(spread, axis=1), jnp.concatenate(hots, axis=1), NT, preferred_element_type=jnp.float32
        )

    def scatter_load(g, loads):
        at = group_at(g)
        high, low = split_two(normals[0, at, :] + normals[1, at, :])
        parts[6, at, :] = high
        parts[7, at, :] = low
        spread, hots = [], []
        for s in range(SUB):
            row = g * SUB + s
            mask = facet_row == wide(slots[pl.ds(row, 1), :] >> 7, 2 * n_rows, jnp.int16)
            both = jnp.where(
                facet_low,
                wide(parts[7, pl.ds(row, 1), :], 2 * n_rows, jnp.bfloat16),
                wide(parts[6, pl.ds(row, 1), :], 2 * n_rows, jnp.bfloat16),
            )
            spread.append(jnp.where(mask, both, jnp.zeros((2 * n_rows, LANES), jnp.bfloat16)))
            hots.append(hot(slots, row))
        return loads + lax.dot_general(
            jnp.concatenate(spread, axis=1), jnp.concatenate(hots, axis=1), NT, preferred_element_type=jnp.float32
        )

    no_push = jnp.zeros((6 * lat, LANES), jnp.float32)

    def add_outer(pushed):
        for c in range(3):
            here = pushed[c * lat : (c + 1) * lat] + pushed[(3 + c) * lat : (4 + c) * lat]
            force[c, rows - lat : rows, :] = force[c, rows - lat : rows, :] + here

    for copy in loads_in[2:5]:
        copy.wait()
    interior(disp)

    def pick_first(g, _):
        for c, x in enumerate(pick(disp, g)):
            picked[c, group_at(g), :] = x
        return 0

    lax.fori_loop(0, groups, pick_first, 0, unroll=8)

    def fill_scale(k, _):
        at = layer_rows(k)
        scale[at, :] = time_step / mass[at, :]
        return 0

    lax.fori_loop(0, layers, fill_scale, 0, unroll=8)

    for copy in loads_in[5:] + own_copies + facet_copies:
        copy.wait()
    for j in range(tiles_need):
        for i in range(half):
            row = tiles[0, j] * half + i
            for a in range(4):
                table[a, j * half + i : j * half + i + 1, :] = facet_all[
                    a * n_road + row // patch_rows, pl.ds(row % patch_rows, 1), :
                ]

    def first_contact(g, pushed):
        at = group_at(g)
        values = pick_facet(g)
        for a in range(4):
            facet_vals[a, at, :] = values[a]
        normals[0, at, :] = press(g, [picked[c, at, :] for c in range(3)], *values)
        return scatter_force(0, g, pushed)

    add_outer(lax.fori_loop(0, groups, first_contact, no_push, unroll=8))

    def advance(k, _):
        at = layer_rows(k)
        for c in range(3):
            v = veloc[c, at, :] + scale[at, :] * (force[c, at, :] + rim_force(k, c))
            v1[c, at, :] = v
            u1[c, at, :] = disp[c, at, :] + time_step * v
        return 0

    for copy in halos0:
        copy.wait()
    fill_rim(0)
    advance(layers - 1, 0)

    lax.fori_loop(0, layers - 1, advance, 0, unroll=5)
    fill_faces(1, u1)
    halos1 = halo_copies(1)
    for copy in halos1:
        copy.start()

    def second_contact(g, loads):
        at = group_at(g)
        normals[1, at, :] = press(g, pick(u1, g), *[facet_vals[a, at, :] for a in range(4)])
        return scatter_load(g, loads)

    loads = lax.fori_loop(0, groups, second_contact, jnp.zeros((2 * n_rows, LANES), jnp.float32), unroll=8)
    loads = loads[:n_rows] + loads[n_rows:]

    spread_rows = n_blk * n_road * load_out.shape[0] if in_kernel_sum else load_out.shape[0]
    row = lax.broadcasted_iota(jnp.int32, (spread_rows, LANES), 0)
    total = jnp.zeros((spread_rows, LANES), jnp.float32)
    for j in range(n_rows):
        total = total + jnp.where(row == tiles[0, j // half] * half + j % half, loads[j : j + 1, :], 0.0)
    if in_kernel_sum:
        chunk_rows = load_out.shape[0]
        for i in range(n_blk * n_road):
            spread_out[i] = total[i * chunk_rows : (i + 1) * chunk_rows]

        @pl.when(b < n_blk - 1)
        def _():
            pl.semaphore_wait(far_sem, (n_blk - 1 - b) * (n_road - 1))

        load_copies = []
        for i in range(1, n_blk * n_road):
            sector = lax.rem(b + i // n_road, n_blk)
            copy = pltpu.make_async_remote_copy(
                src_ref=spread_out.at[sector * n_road + lax.rem(r + i % n_road, n_road)],
                dst_ref=spread_recv.at[i - 1],
                send_sem=spread_sems.at[0, i - 1],
                recv_sem=spread_sems.at[1, i - 1],
                device_id=place(sector, i % n_road),
                device_id_type=MESH,
            )
            copy.start()
            load_copies.append(copy)
    else:
        load_out[...] = total

    interior(u1)
    add_outer(lax.fori_loop(0, groups, functools.partial(scatter_force, 1), no_push, unroll=8))
    for copy in halos1:
        copy.wait()
    fill_rim(1)

    def finish(k, _):
        at = layer_rows(k)
        for c in range(3):
            v_out[c, at, :] = v1[c, at, :] + scale[at, :] * (force[c, at, :] + rim_force(k, c))
        return 0

    lax.fori_loop(0, layers, finish, 0, unroll=8)

    if in_kernel_sum:
        for copy in load_copies:
            copy.wait()
        total = spread_out[b * n_road + r]
        for i in range(n_blk * n_road - 1):
            total = total + spread_recv[i]
        load_out[...] = total


def write_out(v_in, load_in, v_out, load_out, sems):
    copies = [
        pltpu.make_async_copy(src, dst, sems.at[i])
        for i, (src, dst) in enumerate(((v_in, v_out), (load_in, load_out)))
    ]
    for copy in copies:
        copy.start()
    for copy in copies:
        copy.wait()


def on_device(
    n_blk,
    n_road,
    disp,
    veloc,
    stiff,
    mass,
    road_height,
    road_slope_x,
    road_slope_y,
    road_stiff,
    tile_list,
    pair_node,
    pair_slot,
    pair_count,
):
    _, layers, lat, lanes = disp.shape
    rows = layers * lat
    pairs = pair_node.shape[-1]
    pair_rows = pairs // LANES
    tiles_need = tile_list.shape[-1]
    patch_rows = road_height.shape[0] // LANES
    total_rows = patch_rows * n_road
    table_rows = tiles_need * TILE // LANES
    devices = n_blk * n_road
    in_kernel_sum = total_rows % devices == 0
    f32 = jnp.float32
    if in_kernel_sum:
        load_shape = (total_rows // devices, LANES)
    else:
        load_shape = (total_rows, LANES)
    scratch = [
        pltpu.VMEM((3, rows, lanes), f32),
        pltpu.VMEM((3, rows, lanes), f32),
        pltpu.VMEM((3, rows, lanes), f32),
        pltpu.VMEM((rows, lanes), f32),
        pltpu.VMEM((pair_rows, LANES), jnp.int32),
        pltpu.VMEM((pair_rows, LANES), jnp.int32),
        pltpu.SMEM((1, tiles_need), jnp.int32),
        pltpu.SMEM((1,), jnp.int32),
        pltpu.SemaphoreType.DMA((8,)),
        pltpu.SemaphoreType.DMA((4,)),
        pltpu.VMEM((3, pair_rows, LANES), f32),
        pltpu.VMEM((4, pair_rows, LANES), f32),
        pltpu.VMEM((2, pair_rows, LANES), f32),
        pltpu.VMEM((8, pair_rows, LANES), f32),
        pltpu.VMEM((3, rows, lanes), f32),
        pltpu.VMEM((3, rows, lanes), f32),
        pltpu.VMEM((3, rows, lanes), f32),
        pltpu.VMEM((rows, lanes), f32),
        pltpu.VMEM((6, rows // LANES, LANES), f32),
        pltpu.VMEM((6, layers, lanes), f32),
        pltpu.VMEM((4 * n_road, patch_rows, LANES), f32),
        pltpu.VMEM((4, table_rows, LANES), f32),
        pltpu.VMEM((2, 3, rows), f32),
        pltpu.VMEM((2, 4, rows), f32),
        pltpu.VMEM((2, 3, rows), f32),
        pltpu.VMEM((2, 4, rows), f32),
        pltpu.VMEM((2, 3, layers, lanes), f32),
        pltpu.VMEM((2, 4, layers, lanes), f32),
        pltpu.VMEM((2, 3, layers, lanes), f32),
        pltpu.VMEM((2, 4, layers, lanes), f32),
        pltpu.SemaphoreType.DMA((2, 2, 4)),
        pltpu.SemaphoreType.DMA((2, 4, n_road - 1)),
    ]
    if in_kernel_sum:
        scratch += [
            pltpu.VMEM((devices,) + load_shape, f32),
            pltpu.VMEM((devices - 1,) + load_shape, f32),
            pltpu.SemaphoreType.DMA((2, devices - 1)),
            pltpu.SemaphoreType.REGULAR,
            pltpu.SemaphoreType.REGULAR,
        ]
    vmem = pl.BlockSpec(memory_space=pltpu.VMEM)
    hbm = pl.BlockSpec(memory_space=pltpu.HBM)
    anywhere = pl.BlockSpec(memory_space=pl.ANY)
    velocity, load = pl.pallas_call(
        functools.partial(kernel, n_blk, n_road, lat, in_kernel_sum),
        out_shape=(
            pltpu.VMEM((3, rows, lanes), f32),
            pltpu.VMEM(load_shape, f32),
        ),
        in_specs=[hbm] * 12,
        out_specs=(vmem, vmem),
        scratch_shapes=scratch,
        compiler_params=pltpu.CompilerParams(collective_id=0, has_side_effects=True),
    )(
        disp.reshape(3, rows, lanes),
        veloc.reshape(3, rows, lanes),
        stiff.reshape(3, rows, lanes),
        mass.reshape(rows, lanes),
        road_height.reshape(patch_rows, LANES),
        road_slope_x.reshape(patch_rows, LANES),
        road_slope_y.reshape(patch_rows, LANES),
        road_stiff.reshape(patch_rows, LANES),
        tile_list.reshape(1, tiles_need),
        pair_node.reshape(pair_rows, LANES),
        pair_slot.reshape(pair_rows, LANES),
        pair_count.reshape(1,),
    )
    velocity, load = pl.pallas_call(
        write_out,
        out_shape=(
            jax.ShapeDtypeStruct(velocity.shape, f32),
            jax.ShapeDtypeStruct(load.shape, f32),
        ),
        in_specs=[vmem] * 2,
        out_specs=(hbm, hbm),
        scratch_shapes=[pltpu.SemaphoreType.DMA((2,))],
    )(*(pltpu.with_memory_space_constraint(x, pltpu.VMEM) for x in (velocity, load)))
    load = load.reshape(-1)
    if not in_kernel_sum:
        load = lax.psum_scatter(load, ("blk", "road"), scatter_dimension=0, tiled=True)
    return velocity.reshape(disp.shape), load


def solution(mesh):
    in_specs = (
        P(None, None, "road", "blk"),
        P(None, None, "road", "blk"),
        P(None, None, "road", "blk"),
        P(None, "road", "blk"),
        P("road"),
        P("road"),
        P("road"),
        P("road"),
        P("blk", "road", None),
        P("blk", "road", None),
        P("blk", "road", None),
        P("blk", "road"),
    )
    out_specs = (P(None, None, "road", "blk"), P(("blk", "road")))
    body = functools.partial(on_device, mesh.shape["blk"], mesh.shape["road"])
    return jax.shard_map(body, mesh=mesh, in_specs=in_specs, out_specs=out_specs, check_vma=False)
```
